512 devices in a mesh: pipe: 64 (over y, x, core), fsdp: 4 (over z_lo), dp: 2 (over z_hi).
Axes of the slice: x: 4, y: 8, z: 8 (z_hi: 2, z_lo: 4; z = z_hi * 4 + z_lo), core: 2. Of those that a mesh axis runs over, the one named last changes fastest.
Arguments:
- acts: bfloat16 [64, 4, 256, 8192], P('pipe', None, ('fsdp', 'dp')), may hold values from -130 to 130
- cotangent: bfloat16 [64, 4, 256, 512], P('pipe', None, ('fsdp', 'dp')), may hold values from -0.1796875 to 0.1796875
- order: int32 [64, 8, 4], P('pipe', ('fsdp', 'dp')), may hold values from 0 to 3, each once within a row
- key_weight: bfloat16 [64, 8192, 512], P('pipe', 'fsdp'), may hold values from -0.0625 to 0.0625
- gain: float32 [64, 8192], P('pipe', 'fsdp'), may hold values from 0.1 to 1.9
Outputs:
- weight_grad: bfloat16 [64, 8192, 256], P('pipe', ('fsdp', 'dp'))
- gain_grad: float32 [64, 8192], P('pipe', 'fsdp')
The draws below stay inside these ranges and needn't reach their ends.
Inputs may be any that keep to these rules, and one draw needn't show every extreme that they name: Each row of order is a permutation of 0 to 3.
All inputs are finite; a program needn't handle non-finite values.
Results may differ from the reference program's by a relative error of at most 0.0057.
Values may be sent and summed in bfloat16 or wider, within the bound.
No kernel may reach another device: no remote copies, remote signals or barrier semaphores. Data moves between devices by JAX's collectives and lax.ppermute only.
A program may use at most 128 MiB of HBM per device.

```python
import math
import jax
import jax.numpy as jnp
from jax import lax

D = 8192
KV = 512
MB = 4
MB_TOK = 32
ROWS = 256
N_PIPE = 64
N_FSDP = 4
N_DP = 2


def draw_acts(key, part):
    first, second = jax.random.split(key, 2)
    shape = (N_PIPE, MB, ROWS, D)
    base = jnp.clip(jax.random.normal(first, shape, jnp.float32), -5.0, 5.0)
    scales = jnp.exp(jax.random.uniform(second, (N_PIPE, MB, ROWS, 1), jnp.float32, 0.0, math.log(10.0)))
    values = base * scales
    return values.astype(jnp.bfloat16)


def shard_levels(key, extent, pieces, smallest, high):
    def one(dim, shards_of):
        heights = jax.random.uniform(jax.random.fold_in(jax.random.fold_in(key, 6), dim), (shards_of,), jnp.float32, smallest / len(pieces), high / len(pieces))
        return jnp.repeat(jnp.exp(heights), extent[dim] // shards_of).reshape((-1,) + (1,) * (len(extent) - dim - 1))

    level = one(*pieces[0])
    for cut in pieces[1:]:
        level = level * one(*cut)
    return level


def scatter_about(stream_key, shape, width, most, pieces=(), kind=jnp.bfloat16):
    values = jax.random.normal(stream_key, shape, jnp.float32) * width
    if len(pieces) > 0:
        values = shard_levels(stream_key, shape, pieces, -0.22, 0.18) * values
    return jnp.clip(values, min=-most, max=most).astype(kind)


def setup_inputs(seed: int = 0) -> dict:
    streams_of = jax.random.split(jax.random.key(seed), 6)
    acts = draw_acts(jax.random.fold_in(streams_of[5], 71), 0)
    cotangent = scatter_about(streams_of[1], (N_PIPE, MB, ROWS, KV), 0.03, 0.1796875, ((0, 64), (2, 8)))
    order = jax.vmap(lambda own: jax.random.permutation(own, MB))(jax.random.split(streams_of[2], N_PIPE * (N_FSDP * N_DP))).reshape((N_PIPE, N_FSDP * N_DP, MB)).astype(jnp.int32)
    key_weight = scatter_about(streams_of[3], (N_PIPE, D, KV), D ** -0.5, 0.0625, ((0, 64), (1, 4)))
    gain = jnp.clip(1.0 + 0.18 * jax.random.normal(streams_of[4], (N_PIPE, D), jnp.float32), 0.1, 1.9)
    return {"acts": acts, "cotangent": cotangent, "order": order, "key_weight": key_weight, "gain": gain}


def one_rank(inputs):
    values, grads, perm, weight, gain_row = inputs
    floats = values.astype(jnp.float32)
    rstd = lax.rsqrt(lax.optimization_barrier(jnp.mean(floats * floats, axis=-1, keepdims=True)) + 1e-05)
    normed = (floats * rstd).astype(jnp.bfloat16)
    scaled = (normed.astype(jnp.float32) * gain_row).astype(jnp.bfloat16)
    groups = N_FSDP * N_DP
    grads_q = grads.reshape(MB, groups, MB_TOK, KV).astype(jnp.float32)
    onehot = (perm[:, :, None] == jnp.arange(MB, dtype=jnp.int32)[None, None, :]).astype(jnp.float32)
    key_grad = jnp.einsum('qjm,jqtk->mqtk', onehot, grads_q).astype(jnp.bfloat16)
    flat_grad = key_grad.reshape(MB * ROWS, KV)
    flat_scaled = scaled.reshape(MB * ROWS, D)
    flat_normed = normed.reshape(MB * ROWS, D)
    local_w = jnp.dot(flat_scaled.T, flat_grad, preferred_element_type=jnp.float32)
    back = jnp.dot(flat_grad, weight.T, preferred_element_type=jnp.float32)
    local_g = lax.optimization_barrier(jnp.sum(back * flat_normed.astype(jnp.float32), axis=0))
    return (local_w, local_g)

def reference(acts, cotangent, order, key_weight, gain):
    local_w, local_g = lax.map(one_rank, (acts, cotangent, order, key_weight, gain))
    half = KV // 2
    middle = N_PIPE // 2
    paired = local_w + jnp.roll(local_w, middle, axis=0)
    weight_grad = jnp.concatenate([paired[:middle, :, :half], paired[middle:, :, half:]], axis=0).astype(jnp.bfloat16)
    gain_grad = local_g + jnp.roll(local_g, middle, axis=0)
    return (weight_grad, gain_grad)
```

```python
import functools

import jax
import jax.numpy as jnp
from jax import lax
from jax.experimental import pallas as pl
from jax.experimental.pallas import tpu as pltpu
from jax.sharding import PartitionSpec as P

GROUP = ("fsdp", "dp")
CHUNKS = (1024,)
EPS = 1e-05


def split_kernel(groups, chunks, order_ref, acts_ref, cot_ref, first_ref, *rest_refs):
    del order_ref
    width = acts_ref.shape[-1]
    slab = width // groups
    tokens = acts_ref.shape[-2]
    squares = jnp.zeros((tokens, 128), jnp.float32)
    keys = cot_ref.shape[-1]
    for q in range(groups):
        start = q * slab
        for i, rows in enumerate(chunks):
            part = acts_ref[0, 0, :, start : start + rows]
            if i == 0:
                first_ref[q, :, keys:] = part
            else:
                rest_refs[i - 1][q] = part
            floats = part.astype(jnp.float32)
            floats = floats * floats
            for c in range(0, rows, 128):
                squares += floats[:, c : c + 128]
            start += rows
    rstd = lax.rsqrt(jnp.sum(squares, axis=-1, keepdims=True) / width + EPS)
    grads = (cot_ref[0, 0].astype(jnp.float32) * rstd).astype(jnp.bfloat16)
    for q in range(groups):
        first_ref[q, :, :keys] = grads


def split(acts, cotangent, order, groups, chunks):
    _, batches, tokens, width = acts.shape
    keys = cotangent.shape[-1]

    def slot(m, order_ref):
        found = jnp.int32(0)
        for j in range(1, batches):
            found = jnp.where(order_ref[j] == m, jnp.int32(j), found)
        return (0, found, 0, 0)

    sizes = (keys + chunks[0],) + tuple(chunks[1:])
    return pl.pallas_call(
        functools.partial(split_kernel, groups, chunks),
        out_shape=tuple(
            jax.ShapeDtypeStruct((groups, batches * tokens, n), jnp.bfloat16) for n in sizes
        ),
        grid_spec=pltpu.PrefetchScalarGridSpec(
            num_scalar_prefetch=1,
            grid=(batches,),
            in_specs=[
                pl.BlockSpec((1, 1, tokens, width), lambda m, o: (0, m, 0, 0)),
                pl.BlockSpec((1, 1, tokens, keys), slot),
            ],
            out_specs=tuple(
                pl.BlockSpec((groups, tokens, n), lambda m, o: (0, m, 0)) for n in sizes
            ),
        ),
        cost_estimate=pl.CostEstimate(flops=1 << 21, bytes_accessed=5 << 20, transcendentals=128),
        name="split",
    )(order.reshape(-1), acts, cotangent)


def product_kernel(upper_ref, at_ref, acts_ref, grads_ref, weight_ref, gain_ref, keep_ref, send_ref, gterm_ref):
    del at_ref
    total = lax.dot_general(
        acts_ref[...], grads_ref[...], (((0,), (0,)), ((), ())), preferred_element_type=jnp.float32
    )
    rows, keys = total.shape
    terms = total * weight_ref[0].astype(jnp.float32)
    folded = terms[:, :128]
    for c in range(128, keys, 128):
        folded += terms[:, c : c + 128]
    gterm_ref[...] = jnp.sum(folded.T, axis=0, keepdims=True)
    scaled = total * gain_ref[0].reshape(rows, 1)
    half = keys // 2

    @pl.when(upper_ref[0] == 0)
    def _():
        keep_ref[...] = scaled[:, :half]
        send_ref[...] = scaled[:, half:].astype(jnp.bfloat16)

    @pl.when(upper_ref[0] != 0)
    def _():
        keep_ref[...] = scaled[:, half:]
        send_ref[...] = scaled[:, :half].astype(jnp.bfloat16)


def product(upper, replica, acts, skip, grads_from, weight, gain, offset, rows, slab):
    tokens = acts.shape[0]
    keys = weight.shape[-1]
    tile = 256
    first = (replica * slab + offset) // tile
    return pl.pallas_call(
        product_kernel,
        out_shape=(
            jax.ShapeDtypeStruct((rows, keys // 2), jnp.float32),
            jax.ShapeDtypeStruct((rows, keys // 2), jnp.bfloat16),
            jax.ShapeDtypeStruct((1, rows), jnp.float32),
        ),
        grid_spec=pltpu.PrefetchScalarGridSpec(
            num_scalar_prefetch=2,
            grid=(rows // tile,),
            in_specs=[
                pl.BlockSpec((tokens, tile), lambda i, u, a: (0, skip // tile + i)),
                pl.BlockSpec((tokens, keys), lambda i, u, a: (0, 0)),
                pl.BlockSpec((1, tile, keys), lambda i, u, a: (0, a[0] + i, 0)),
                pl.BlockSpec((1, tile), lambda i, u, a: (0, a[0] + i)),
            ],
            out_specs=(
                pl.BlockSpec((tile, keys // 2), lambda i, u, a: (i, 0)),
                pl.BlockSpec((tile, keys // 2), lambda i, u, a: (i, 0)),
                pl.BlockSpec((1, tile), lambda i, u, a: (0, i)),
            ),
        ),
        cost_estimate=pl.CostEstimate(
            flops=2 * tokens * rows * keys,
            bytes_accessed=2 * tokens * (rows + keys) + 4 * rows * keys,
            transcendentals=0,
        ),
        name="product",
    )(upper, first.reshape(1), acts, grads_from, weight, gain)


def local(acts, cotangent, order, key_weight, gain):
    groups = lax.axis_size(GROUP)
    width = acts.shape[-1]
    slab = width // groups
    keys = cotangent.shape[-1]
    tokens = acts.shape[1] * acts.shape[2]
    ranks = lax.axis_size("pipe")
    middle = ranks // 2
    upper = (lax.axis_index("pipe") >= middle).astype(jnp.int32).reshape(1)
    replica = lax.axis_index("dp")
    across = [(i, (i + middle) % ranks) for i in range(ranks)]
    copies = lax.axis_size("dp")
    beside = [(i, (i + 1) % copies) for i in range(copies)]

    sent = split(acts, cotangent, order, groups, CHUNKS)
    got = [lax.all_to_all(block, GROUP, 0, 0, tiled=True) for block in sent]
    got = [block.reshape(groups * tokens, block.shape[-1]) for block in got]
    offset = 0
    kept, arrived, gterms = [], [], []
    for i, (block, rows) in enumerate(zip(got, CHUNKS)):
        skip = keys if i == 0 else 0
        keep, send, gterm = product(
            upper, replica, block, skip, got[0], key_weight, gain, offset, rows, slab
        )
        kept.append(keep)
        arrived.append(lax.ppermute(send, "pipe", across))
        gterms.append(gterm)
        offset += rows
    gown = jnp.concatenate(gterms, axis=1)
    gpair = gown + lax.ppermute(gown, "pipe", across)
    gbeside = lax.ppermute(gpair, "dp", beside)
    gain_pair = jnp.where(
        replica == 0,
        jnp.concatenate([gpair, gbeside], axis=1),
        jnp.concatenate([gbeside, gpair], axis=1),
    )
    weight_out = jnp.concatenate(
        [(keep + block).astype(jnp.bfloat16) for keep, block in zip(kept, arrived)], axis=0
    )
    return (weight_out[None], gain_pair)


def solution(mesh):
    return jax.shard_map(
        local,
        mesh=mesh,
        in_specs=(
            P("pipe", None, GROUP, None),
            P("pipe", None, GROUP, None),
            P("pipe", GROUP, None),
            P("pipe", "fsdp", None),
            P("pipe", "fsdp"),
        ),
        out_specs=(P("pipe", GROUP, None), P("pipe", "fsdp")),
        check_vma=False,
    )
```

```python
import functools

import jax
import jax.numpy as jnp
from jax import lax
from jax.experimental import pallas as pl
from jax.experimental.pallas import tpu as pltpu
from jax.sharding import PartitionSpec as P

GROUP = ("fsdp", "dp")
TILE = 128
EPS = 1e-05
ADDCOST = 1 << 20
VLIM = 20
HBM = pl.BlockSpec(memory_space=pltpu.HBM)
VMEM = pl.BlockSpec(memory_space=pltpu.VMEM)
SMEM = pl.BlockSpec(memory_space=pltpu.SMEM)


def params():
    return pltpu.CompilerParams(vmem_limit_bytes=VLIM << 20)


def cost(size=0):
    return pl.CostEstimate(flops=0, bytes_accessed=size, transcendentals=0)


def split_kernel(
    order_ref, upper_ref, acts_ref, cot_ref, first_ref, second_ref,
    acts_own, cot_own, send_own, keep_own, acts_sem, cot_sem, move_sem, send_sem, keep_sem,
):
    groups = first_ref.shape[0]
    _, batches, tokens, width = acts_ref.shape
    slab = width // groups
    half = cot_ref.shape[-1] // 2
    load_cot = pltpu.make_async_copy(cot_ref.at[0], cot_own, cot_sem)
    load_cot.start()
    loads, moves = [], []
    for m in range(batches):
        loads.append(pltpu.make_async_copy(acts_ref.at[0, m], acts_own.at[m], acts_sem.at[m]))
        loads[-1].start()
    load_cot.wait()
    keep_at = pl.multiple_of(upper_ref[0] * half, 128)
    send_at = pl.multiple_of((1 - upper_ref[0]) * half, 128)
    for m in range(batches):
        loads[m].wait()
        for q in range(groups):
            moves.append(
                pltpu.make_async_copy(
                    acts_own.at[m, :, pl.ds(q * slab, slab)],
                    first_ref.at[q, pl.ds(m * tokens, tokens), pl.ds(half, slab)],
                    move_sem.at[m, q],
                )
            )
            moves[-1].start()
        squares = jnp.zeros((tokens, 128), jnp.float32)
        for c in range(0, width, 128):
            part = acts_own[m, :, c : c + 128].astype(jnp.float32)
            squares += part * part
        rstd = lax.rsqrt(jnp.sum(squares, axis=-1, keepdims=True) / width + EPS)
        slot = jnp.int32(0)
        for j in range(1, batches):
            slot = jnp.where(order_ref[j] == m, jnp.int32(j), slot)
        rows = pl.ds(m * tokens, tokens)
        send_own[rows, :] = (cot_own[slot, :, pl.ds(send_at, half)].astype(jnp.float32) * rstd).astype(jnp.bfloat16)
        keep_own[rows, :] = (cot_own[slot, :, pl.ds(keep_at, half)].astype(jnp.float32) * rstd).astype(jnp.bfloat16)
    for q in range(groups):
        moves.append(pltpu.make_async_copy(send_own, first_ref.at[q, :, pl.ds(0, half)], send_sem.at[q]))
        moves[-1].start()
        moves.append(pltpu.make_async_copy(keep_own, second_ref.at[q], keep_sem.at[q]))
        moves[-1].start()
    for move in moves:
        move.wait()


def split(acts, cotangent, order, upper, groups):
    _, batches, tokens, width = acts.shape
    keys = cotangent.shape[-1]
    half = keys // 2
    sizes = (half + width // groups, half)
    dma = pltpu.SemaphoreType.DMA
    return pl.pallas_call(
        split_kernel,
        out_shape=tuple(jax.ShapeDtypeStruct((groups, batches * tokens, n), jnp.bfloat16) for n in sizes),
        in_specs=[SMEM, SMEM, HBM, HBM],
        out_specs=(HBM, HBM),
        scratch_shapes=[
            pltpu.VMEM((batches, tokens, width), jnp.bfloat16),
            pltpu.VMEM((batches, tokens, keys), jnp.bfloat16),
            pltpu.VMEM((batches * tokens, half), jnp.bfloat16),
            pltpu.VMEM((batches * tokens, half), jnp.bfloat16),
            dma((batches,)),
            dma,
            dma((batches, groups)),
            dma((groups,)),
            dma((groups,)),
        ],
        cost_estimate=cost(5 << 20),
        name="split",
    )(order.reshape(-1), upper, acts, cotangent)


def half_product(block_ref, grads, at, half):
    return lax.dot_general(
        block_ref[:, half + at : half + at + TILE], grads, (((0,), (0,)), ((), ())), preferred_element_type=jnp.float32
    )


def gain_terms(total, weight):
    terms = total * weight.astype(jnp.float32)
    folded = terms[:, :128]
    for c in range(128, terms.shape[1], 128):
        folded += terms[:, c : c + 128]
    return jnp.sum(folded.T, axis=0, keepdims=True)


def fetch_weight(weight_ref, own_ref, sem, first, column):
    rows, half = own_ref.shape
    copy = pltpu.make_async_copy(weight_ref.at[0, pl.ds(first, rows), pl.ds(column, half)], own_ref, sem)
    copy.start()
    return copy


def send_kernel(upper_ref, replica_ref, block_ref, weight_ref, gain_ref, send_ref, gterm_ref, own_ref, total_ref, sem):
    rows, half = own_ref.shape
    first = pl.multiple_of(replica_ref[0] * rows, rows)
    fetch = fetch_weight(weight_ref, own_ref, sem, first, pl.multiple_of((1 - upper_ref[0]) * half, half))
    grads = block_ref[:, :half]
    for at in range(0, rows, TILE):
        total = half_product(block_ref, grads, at, half)
        gain = gain_ref[:, pl.ds(pl.multiple_of(first + at, 128), TILE)].reshape(TILE, 1)
        send_ref[at : at + TILE, :] = (total * gain).astype(jnp.bfloat16)
        total_ref[at : at + TILE, :] = total
    fetch.wait()
    for at in range(0, rows, TILE):
        gterm_ref[:, at : at + TILE] = gain_terms(total_ref[at : at + TILE, :], own_ref[at : at + TILE, :])


def gain_kernel(upper_ref, replica_ref, before_ref, grads_ref, block_ref, weight_ref, gterm_ref, own_ref, total_ref, sem):
    rows, half = own_ref.shape
    first = pl.multiple_of(replica_ref[0] * rows, rows)
    fetch = fetch_weight(weight_ref, own_ref, sem, first, pl.multiple_of(upper_ref[0] * half, half))
    gterm_ref[...] = jnp.zeros_like(gterm_ref)
    grads = grads_ref[...]
    for at in range(0, rows, TILE):
        total_ref[at : at + TILE, :] = half_product(block_ref, grads, at, half)
    fetch.wait()
    for at in range(0, rows, TILE):
        gterm = gain_terms(total_ref[at : at + TILE, :], own_ref[at : at + TILE, :])
        gterm_ref[:, pl.ds(pl.multiple_of(first + at, 128), TILE)] = gterm + before_ref[:, at : at + TILE]


def finish_kernel(replica_ref, grads_ref, block_ref, gain_ref, arrived_ref, out_ref):
    rows, half = arrived_ref.shape
    first = pl.multiple_of(replica_ref[0] * rows, rows)
    grads = grads_ref[...]
    for at in range(0, rows, TILE):
        gain = gain_ref[:, pl.ds(pl.multiple_of(first + at, 128), TILE)].reshape(TILE, 1)
        keep = half_product(block_ref, grads, at, half) * gain
        out_ref[0, at : at + TILE, :] = (keep + arrived_ref[at : at + TILE, :].astype(jnp.float32)).astype(jnp.bfloat16)


def local(acts, cotangent, order, key_weight, gain):
    groups = lax.axis_size(GROUP)
    slab = acts.shape[-1] // groups
    tokens = acts.shape[1] * acts.shape[2]
    half = cotangent.shape[-1] // 2
    ranks = lax.axis_size("pipe")
    middle = ranks // 2
    upper = (lax.axis_index("pipe") >= middle).astype(jnp.int32).reshape(1)
    replica = lax.axis_index("dp").reshape(1)
    across = [(i, (i + middle) % ranks) for i in range(ranks)]
    pairs = [[i, i + middle] for i in range(middle)]

    def exchange(block):
        return lax.all_to_all(block, GROUP, 0, 0, tiled=True).reshape(groups * tokens, -1)

    key_weight = pltpu.with_memory_space_constraint(key_weight, pltpu.HBM)
    first, second = split(acts, cotangent, order, upper, groups)
    block = exchange(first)
    second, block = lax.optimization_barrier((second, block))
    grads = exchange(second)
    scratch = [
        pltpu.VMEM((slab, half), jnp.bfloat16),
        pltpu.VMEM((slab, half), jnp.float32),
        pltpu.SemaphoreType.DMA,
    ]
    send, gterm = pl.pallas_call(
        send_kernel,
        out_shape=(jax.ShapeDtypeStruct((slab, half), jnp.bfloat16), jax.ShapeDtypeStruct((1, slab), jnp.float32)),
        in_specs=[SMEM, SMEM, VMEM, HBM, VMEM],
        out_specs=(VMEM, VMEM),
        scratch_shapes=scratch,
        cost_estimate=cost(),
        compiler_params=params(),
        name="send",
    )(upper, replica, block, key_weight, gain)
    arrived = lax.ppermute(send, "pipe", across)
    gown = pl.pallas_call(
        gain_kernel,
        out_shape=jax.ShapeDtypeStruct(gain.shape, jnp.float32),
        in_specs=[SMEM, SMEM, VMEM, VMEM, VMEM, HBM],
        out_specs=VMEM,
        scratch_shapes=scratch,
        cost_estimate=cost(),
        compiler_params=params(),
        name="gain",
    )(upper, replica, gterm, grads, block, key_weight)
    gain_pair = lax.psum(lax.psum(gown, "dp"), "pipe", axis_index_groups=pairs)
    weight_out = pl.pallas_call(
        finish_kernel,
        out_shape=jax.ShapeDtypeStruct((1, slab, half), jnp.bfloat16),
        in_specs=[SMEM, VMEM, VMEM, VMEM, VMEM],
        out_specs=VMEM,
        cost_estimate=cost(ADDCOST),
        compiler_params=params(),
        name="finish",
    )(replica, grads, block, gain, arrived)
    return (weight_out, gain_pair)


def solution(mesh):
    return jax.shard_map(
        local,
        mesh=mesh,
        in_specs=(
            P("pipe", None, GROUP, None),
            P("pipe", None, GROUP, None),
            P("pipe", GROUP, None),
            P("pipe", "fsdp", None),
            P("pipe", "fsdp"),
        ),
        out_specs=(P("pipe", GROUP, None), P("pipe", "fsdp")),
        check_vma=False,
    )
```

```python
import functools

import jax
import jax.numpy as jnp
from jax import lax
from jax.experimental import pallas as pl
from jax.experimental.pallas import tpu as pltpu
from jax.sharding import PartitionSpec as P

GROUP = ("fsdp", "dp")
TILE = 256
SPLIT = 80
STEPS = 4
EPS = 1e-05
ADDCOST = 1 << 20
VLIM = 20
HBM = pl.BlockSpec(memory_space=pltpu.HBM)
VMEM = pl.BlockSpec(memory_space=pltpu.VMEM)
SMEM = pl.BlockSpec(memory_space=pltpu.SMEM)
ARRIVED = pl.BlockSpec(memory_space=pl.ANY)


def params():
    return pltpu.CompilerParams(vmem_limit_bytes=VLIM << 20)


def cost(size=0):
    return pl.CostEstimate(flops=0, bytes_accessed=size, transcendentals=0)


def split_kernel(
    order_ref, upper_ref, acts_ref, cot_ref, first_ref, second_ref,
    acts_own, cot_own, keep_own, acts_sem, cot_sem, keep_sem,
):
    groups = first_ref.shape[0]
    _, batches, tokens, width = acts_ref.shape
    slab = width // groups
    half = cot_ref.shape[-1] // 2
    copies = [pltpu.make_async_copy(acts_ref.at[0, m], acts_own.at[m], acts_sem.at[m]) for m in range(batches)]
    load_cot = pltpu.make_async_copy(cot_ref.at[0], cot_own, cot_sem)
    for load in copies:
        load.start()
    load_cot.start()
    keep_at = pl.multiple_of(upper_ref[0] * half, 128)
    send_at = pl.multiple_of((1 - upper_ref[0]) * half, 128)
    stores = []
    for m in range(batches):
        copies[m].wait()
        rows = slice(m * tokens, (m + 1) * tokens)
        squares = jnp.zeros((tokens, 128), jnp.float32)
        for c in range(0, width, 128):
            floats = acts_own[m, :, c : c + 128].astype(jnp.float32)
            squares += floats * floats
        rstd = lax.rsqrt(jnp.sum(squares, axis=-1, keepdims=True) / width + EPS)
        if m == 0:
            load_cot.wait()
        slot = jnp.int32(0)
        for j in range(1, batches):
            slot = jnp.where(order_ref[0, 0, j] == m, jnp.int32(j), slot)
        send = (cot_own[slot, :, pl.ds(send_at, half)].astype(jnp.float32) * rstd).astype(jnp.bfloat16)
        keep = (cot_own[slot, :, pl.ds(keep_at, half)].astype(jnp.float32) * rstd).astype(jnp.bfloat16)
        for q in range(groups):
            keep_own[q, rows, :] = keep
        stores.append(pltpu.make_async_copy(keep_own.at[:, rows], second_ref.at[:, rows], keep_sem.at[m]))
        stores[-1].start()
        for q in range(groups):
            first_ref[q, rows, :half] = send
            first_ref[q, rows, half:] = acts_own[m, :, q * slab : (q + 1) * slab]
    for store in stores:
        store.wait()


def split(acts, cotangent, order, upper, groups):
    _, batches, tokens, width = acts.shape
    keys = cotangent.shape[-1]
    half = keys // 2
    sizes = (half + width // groups, half)
    acts, cotangent, order = (pltpu.with_memory_space_constraint(x, pltpu.HBM) for x in (acts, cotangent, order))
    return pl.pallas_call(
        split_kernel,
        out_shape=tuple(jax.ShapeDtypeStruct((groups, batches * tokens, n), jnp.bfloat16) for n in sizes),
        in_specs=[SMEM, SMEM, HBM, HBM],
        out_specs=(VMEM, HBM),
        scratch_shapes=[
            pltpu.VMEM((batches, tokens, width), jnp.bfloat16),
            pltpu.VMEM((batches, tokens, keys), jnp.bfloat16),
            pltpu.VMEM((groups, batches * tokens, half), jnp.bfloat16),
            pltpu.SemaphoreType.DMA((batches,)),
            pltpu.SemaphoreType.DMA,
            pltpu.SemaphoreType.DMA((batches,)),
        ],
        cost_estimate=cost(5 << 20),
        compiler_params=pltpu.CompilerParams(vmem_limit_bytes=SPLIT << 18),
        name="split",
    )(order, upper, acts, cotangent)


def half_product(block_ref, grads, at, half):
    return lax.dot_general(
        block_ref[:, half + at : half + at + TILE], grads, (((0,), (0,)), ((), ())), preferred_element_type=jnp.float32
    )


def gain_terms(total, weight):
    terms = total * weight.astype(jnp.float32)
    folded = terms[:, :128]
    for c in range(128, terms.shape[1], 128):
        folded += terms[:, c : c + 128]
    return jnp.sum(folded.T, axis=0, keepdims=True)


def fetch_weight(weight_ref, own_ref, sem, first, column):
    rows, half = own_ref.shape
    copy = pltpu.make_async_copy(weight_ref.at[0, pl.ds(first, rows), pl.ds(column, half)], own_ref, sem)
    copy.start()
    return copy


def send_kernel(upper_ref, replica_ref, block_ref, weight_ref, gain_ref, send_ref, gterm_ref, own_ref, total_ref, sem):
    rows, half = own_ref.shape
    first = pl.multiple_of(replica_ref[0] * rows, rows)
    fetch = fetch_weight(weight_ref, own_ref, sem, first, pl.multiple_of((1 - upper_ref[0]) * half, half))
    grads = block_ref[:, :half]
    for at in range(0, rows, TILE):
        total = half_product(block_ref, grads, at, half)
        gain = gain_ref[:, pl.ds(pl.multiple_of(first + at, 128), TILE)].reshape(TILE, 1)
        send_ref[at : at + TILE, :] = (total * gain).astype(jnp.bfloat16)
        total_ref[at : at + TILE, :] = total
    fetch.wait()
    for at in range(0, rows, TILE):
        gterm_ref[:, at : at + TILE] = gain_terms(total_ref[at : at + TILE, :], own_ref[at : at + TILE, :])


def gain_kernel(upper_ref, replica_ref, before_ref, grads_ref, block_ref, weight_ref, gterm_ref, own_ref, total_ref, sem):
    rows, half = own_ref.shape
    first = pl.multiple_of(replica_ref[0] * rows, rows)
    fetch = fetch_weight(weight_ref, own_ref, sem, first, pl.multiple_of(upper_ref[0] * half, half))
    gterm_ref[...] = jnp.zeros_like(gterm_ref)
    grads = grads_ref[...]
    for at in range(0, rows, TILE):
        total_ref[at : at + TILE, :] = half_product(block_ref, grads, at, half)
    fetch.wait()
    for at in range(0, rows, TILE):
        gterm = gain_terms(total_ref[at : at + TILE, :], own_ref[at : at + TILE, :])
        gterm_ref[:, pl.ds(pl.multiple_of(first + at, 128), TILE)] = gterm + before_ref[:, at : at + TILE]


def keep_kernel(replica_ref, after_ref, grads_ref, block_ref, gain_ref, keep_ref):
    del after_ref
    rows, half = keep_ref.shape
    first = pl.multiple_of(replica_ref[0] * rows, rows)
    grads = grads_ref[...]
    for at in range(0, rows, TILE):
        gain = gain_ref[:, pl.ds(pl.multiple_of(first + at, 128), TILE)].reshape(TILE, 1)
        keep_ref[at : at + TILE, :] = half_product(block_ref, grads, at, half) * gain


def add_kernel(keep_ref, arrived_ref, out_ref, arrived_own, out_own, load_sem, store_sem):
    rows = keep_ref.shape[0] // STEPS
    bands = [pl.ds(n * rows, rows) for n in range(STEPS)]
    loads = [
        pltpu.make_async_copy(arrived_ref.at[band], arrived_own.at[band], load_sem.at[n]) for n, band in enumerate(bands)
    ]
    stores = [
        pltpu.make_async_copy(out_own.at[band], out_ref.at[0, band], store_sem.at[n]) for n, band in enumerate(bands)
    ]
    for load in loads:
        load.start()
    for band, load, store in zip(bands, loads, stores):
        load.wait()
        out_own[band, :] = (keep_ref[band, :] + arrived_own[band, :].astype(jnp.float32)).astype(jnp.bfloat16)
        store.start()
    for store in stores:
        store.wait()


def local(acts, cotangent, order, key_weight, gain):
    groups = lax.axis_size(GROUP)
    slab = acts.shape[-1] // groups
    tokens = acts.shape[1] * acts.shape[2]
    half = cotangent.shape[-1] // 2
    ranks = lax.axis_size("pipe")
    middle = ranks // 2
    upper = (lax.axis_index("pipe") >= middle).astype(jnp.int32).reshape(1)
    replica = lax.axis_index("dp").reshape(1)
    across = [(i, (i + middle) % ranks) for i in range(ranks)]

    def exchange(block):
        return lax.all_to_all(block, GROUP, 0, 0, tiled=True).reshape(groups * tokens, -1)

    key_weight = pltpu.with_memory_space_constraint(key_weight, pltpu.HBM)
    first, second = split(acts, cotangent, order, upper, groups)
    block = exchange(first)
    second, block = lax.optimization_barrier((second, block))
    grads = exchange(second)
    scratch = [
        pltpu.VMEM((slab, half), jnp.bfloat16),
        pltpu.VMEM((slab, half), jnp.float32),
        pltpu.SemaphoreType.DMA,
    ]
    send, gterm = pl.pallas_call(
        send_kernel,
        out_shape=(jax.ShapeDtypeStruct((slab, half), jnp.bfloat16), jax.ShapeDtypeStruct((1, slab), jnp.float32)),
        in_specs=[SMEM, SMEM, VMEM, HBM, VMEM],
        out_specs=(VMEM, VMEM),
        scratch_shapes=scratch,
        cost_estimate=cost(),
        compiler_params=params(),
        name="send",
    )(upper, replica, block, key_weight, gain)
    arrived = lax.ppermute(send, "pipe", across)
    gown = pl.pallas_call(
        gain_kernel,
        out_shape=jax.ShapeDtypeStruct(gain.shape, jnp.float32),
        in_specs=[SMEM, SMEM, VMEM, VMEM, VMEM, HBM],
        out_specs=VMEM,
        scratch_shapes=scratch,
        cost_estimate=cost(),
        compiler_params=params(),
        name="gain",
    )(upper, replica, gterm, grads, block, key_weight)
    gboth = gown + lax.ppermute(gown, "dp", [(0, 1), (1, 0)])
    there = lax.ppermute(gboth, "pipe", across)
    keep = pl.pallas_call(
        keep_kernel,
        out_shape=jax.ShapeDtypeStruct((slab, half), jnp.float32),
        in_specs=[SMEM, pl.BlockSpec(memory_space=pl.ANY), VMEM, VMEM, VMEM],
        out_specs=VMEM,
        cost_estimate=cost(),
        compiler_params=params(),
        name="keep",
    )(replica, gboth, grads, block, gain)
    weight_out = pl.pallas_call(
        add_kernel,
        out_shape=jax.ShapeDtypeStruct((1, slab, half), jnp.bfloat16),
        in_specs=[VMEM, ARRIVED],
        out_specs=HBM,
        scratch_shapes=[
            pltpu.VMEM((slab, half), jnp.bfloat16),
            pltpu.VMEM((slab, half), jnp.bfloat16),
            pltpu.SemaphoreType.DMA((STEPS,)),
            pltpu.SemaphoreType.DMA((STEPS,)),
        ],
        cost_estimate=cost(ADDCOST),
        compiler_params=params(),
        name="add",
    )(keep, arrived)
    return (weight_out, gboth + there)


def solution(mesh):
    return jax.shard_map(
        local,
        mesh=mesh,
        in_specs=(
            P("pipe", None, GROUP, None),
            P("pipe", None, GROUP, None),
            P("pipe", GROUP, None),
            P("pipe", "fsdp", None),
            P("pipe", "fsdp"),
        ),
        out_specs=(P("pipe", GROUP, None), P("pipe", "fsdp")),
        check_vma=False,
    )
```

```python
import functools

import jax
import jax.numpy as jnp
from jax import lax
from jax.experimental import pallas as pl
from jax.experimental.pallas import tpu as pltpu
from jax.sharding import PartitionSpec as P

GROUP = ("fsdp", "dp")
TILE = 256
SPLIT = 80
STEPS = 4
EPS = 1e-05
ADDCOST = 1 << 20
VLIM = 20
HBM = pl.BlockSpec(memory_space=pltpu.HBM)
VMEM = pl.BlockSpec(memory_space=pltpu.VMEM)
SMEM = pl.BlockSpec(memory_space=pltpu.SMEM)
ARRIVED = pl.BlockSpec(memory_space=pl.ANY)


def params():
    return pltpu.CompilerParams(vmem_limit_bytes=VLIM << 20)


def cost(size=0):
    return pl.CostEstimate(flops=0, bytes_accessed=size, transcendentals=0)


def split_kernel(
    order_ref, upper_ref, acts_ref, cot_ref, first_ref, second_ref, acts_own, cot_own, acts_sem, cot_sem
):
    groups = first_ref.shape[0]
    _, batches, tokens, width = acts_ref.shape
    slab = width // groups
    half = cot_ref.shape[-1] // 2
    copies = [pltpu.make_async_copy(acts_ref.at[0, m], acts_own.at[m], acts_sem.at[m]) for m in range(batches)]
    load_cot = pltpu.make_async_copy(cot_ref.at[0], cot_own, cot_sem)
    for load in copies:
        load.start()
    load_cot.start()
    keep_at = pl.multiple_of(upper_ref[0] * half, 128)
    send_at = pl.multiple_of((1 - upper_ref[0]) * half, 128)
    for m in range(batches):
        copies[m].wait()
        rows = slice(m * tokens, (m + 1) * tokens)
        squares = jnp.zeros((tokens, 128), jnp.float32)
        for c in range(0, width, 128):
            floats = acts_own[m, :, c : c + 128].astype(jnp.float32)
            squares += floats * floats
        rstd = lax.rsqrt(jnp.sum(squares, axis=-1, keepdims=True) / width + EPS)
        if m == 0:
            load_cot.wait()
        slot = jnp.int32(0)
        for j in range(1, batches):
            slot = jnp.where(order_ref[0, 0, j] == m, jnp.int32(j), slot)
        send = (cot_own[slot, :, pl.ds(send_at, half)].astype(jnp.float32) * rstd).astype(jnp.bfloat16)
        keep = (cot_own[slot, :, pl.ds(keep_at, half)].astype(jnp.float32) * rstd).astype(jnp.bfloat16)
        for q in range(groups):
            second_ref[q, rows, :] = keep
            first_ref[q, rows, :half] = send
            first_ref[q, rows, half:] = acts_own[m, :, q * slab : (q + 1) * slab]


def split(acts, cotangent, order, upper, groups):
    _, batches, tokens, width = acts.shape
    keys = cotangent.shape[-1]
    half = keys // 2
    sizes = (half + width // groups, half)
    acts, cotangent, order = (pltpu.with_memory_space_constraint(x, pltpu.HBM) for x in (acts, cotangent, order))
    return pl.pallas_call(
        split_kernel,
        out_shape=tuple(jax.ShapeDtypeStruct((groups, batches * tokens, n), jnp.bfloat16) for n in sizes),
        in_specs=[SMEM, SMEM, HBM, HBM],
        out_specs=(VMEM, VMEM),
        scratch_shapes=[
            pltpu.VMEM((batches, tokens, width), jnp.bfloat16),
            pltpu.VMEM((batches, tokens, keys), jnp.bfloat16),
            pltpu.SemaphoreType.DMA((batches,)),
            pltpu.SemaphoreType.DMA,
        ],
        cost_estimate=cost(5 << 20),
        compiler_params=pltpu.CompilerParams(vmem_limit_bytes=SPLIT << 18),
        name="split",
    )(order, upper, acts, cotangent)


def half_product(block_ref, grads, at, half):
    return lax.dot_general(
        block_ref[:, half + at : half + at + TILE], grads, (((0,), (0,)), ((), ())), preferred_element_type=jnp.float32
    )


def gain_terms(total, weight):
    terms = total * weight.astype(jnp.float32)
    folded = terms[:, :128]
    for c in range(128, terms.shape[1], 128):
        folded += terms[:, c : c + 128]
    return jnp.sum(folded.T, axis=0, keepdims=True)


def fetch_weight(weight_ref, own_ref, sem, first, column):
    rows, half = own_ref.shape
    copy = pltpu.make_async_copy(weight_ref.at[0, pl.ds(first, rows), pl.ds(column, half)], own_ref, sem)
    copy.start()
    return copy


def scaled_kernel(replica_ref, grads_ref, block_ref, gain_ref, out_ref):
    rows, half = out_ref.shape
    first = pl.multiple_of(replica_ref[0] * rows, rows)
    grads = grads_ref[:, :half]
    for at in range(0, rows, TILE):
        gain = gain_ref[:, pl.ds(pl.multiple_of(first + at, 128), TILE)].reshape(TILE, 1)
        out_ref[at : at + TILE, :] = (half_product(block_ref, grads, at, half) * gain).astype(out_ref.dtype)


def gain_kernel(keeping, upper_ref, replica_ref, grads_ref, block_ref, weight_ref, *refs):
    before, (gterm_ref, own_ref, total_ref, sem) = refs[:keeping], refs[keeping:]
    rows, half = own_ref.shape
    first = pl.multiple_of(replica_ref[0] * rows, rows)
    side = upper_ref[0] if keeping else 1 - upper_ref[0]
    fetch = fetch_weight(weight_ref, own_ref, sem, first, pl.multiple_of(side * half, half))
    if keeping:
        gterm_ref[...] = jnp.zeros_like(gterm_ref)
    grads = grads_ref[:, :half]
    for at in range(0, rows, TILE):
        total_ref[at : at + TILE, :] = half_product(block_ref, grads, at, half)
    fetch.wait()
    for at in range(0, rows, TILE):
        gterm = gain_terms(total_ref[at : at + TILE, :], own_ref[at : at + TILE, :])
        if keeping:
            where = pl.ds(pl.multiple_of(first + at, 128), TILE)
            gterm_ref[:, where] = gterm + before[0][:, at : at + TILE]
        else:
            gterm_ref[:, at : at + TILE] = gterm


def add_kernel(keep_ref, arrived_ref, out_ref, arrived_own, out_own, load_sem, store_sem):
    rows = keep_ref.shape[0] // STEPS
    bands = [pl.ds(n * rows, rows) for n in range(STEPS)]
    loads = [
        pltpu.make_async_copy(arrived_ref.at[band], arrived_own.at[band], load_sem.at[n]) for n, band in enumerate(bands)
    ]
    stores = [
        pltpu.make_async_copy(out_own.at[band], out_ref.at[0, band], store_sem.at[n]) for n, band in enumerate(bands)
    ]
    for load in loads:
        load.start()
    for band, load, store in zip(bands, loads, stores):
        load.wait()
        out_own[band, :] = (keep_ref[band, :] + arrived_own[band, :].astype(jnp.float32)).astype(jnp.bfloat16)
        store.start()
    for store in stores:
        store.wait()


def local(acts, cotangent, order, key_weight, gain):
    groups = lax.axis_size(GROUP)
    slab = acts.shape[-1] // groups
    tokens = acts.shape[1] * acts.shape[2]
    half = cotangent.shape[-1] // 2
    ranks = lax.axis_size("pipe")
    middle = ranks // 2
    upper = (lax.axis_index("pipe") >= middle).astype(jnp.int32).reshape(1)
    replica = lax.axis_index("dp").reshape(1)
    across = [(i, (i + middle) % ranks) for i in range(ranks)]

    def exchange(block):
        return lax.all_to_all(block, GROUP, 0, 0, tiled=True).reshape(groups * tokens, -1)

    key_weight = pltpu.with_memory_space_constraint(key_weight, pltpu.HBM)
    first, second = split(acts, cotangent, order, upper, groups)
    block = exchange(first)
    second, block = lax.optimization_barrier((second, block))
    grads = exchange(second)
    scratch = [
        pltpu.VMEM((slab, half), jnp.bfloat16),
        pltpu.VMEM((slab, half), jnp.float32),
        pltpu.SemaphoreType.DMA,
    ]

    def scaled(grads, kind, name):
        return pl.pallas_call(
            scaled_kernel,
            out_shape=jax.ShapeDtypeStruct((slab, half), kind),
            in_specs=[SMEM, VMEM, VMEM, VMEM],
            out_specs=VMEM,
            cost_estimate=cost(),
            compiler_params=params(),
            name=name,
        )(replica, grads, block, gain)

    def gain_part(grads, *before):
        return pl.pallas_call(
            functools.partial(gain_kernel, len(before)),
            out_shape=jax.ShapeDtypeStruct(gain.shape if before else (1, slab), jnp.float32),
            in_specs=[SMEM, SMEM, VMEM, VMEM, HBM] + [VMEM] * len(before),
            out_specs=VMEM,
            scratch_shapes=scratch,
            cost_estimate=cost(),
            compiler_params=params(),
            name="gain",
        )(upper, replica, grads, block, key_weight, *before)

    arrived = lax.ppermute(scaled(block, jnp.bfloat16, "send"), "pipe", across)
    gown = gain_part(grads, gain_part(block))
    gboth = lax.psum(gown, "dp")
    there = lax.ppermute(gboth, "pipe", across)
    late_grads, _ = lax.optimization_barrier((grads, gboth))
    keep = scaled(late_grads, jnp.float32, "keep")
    weight_out = pl.pallas_call(
        add_kernel,
        out_shape=jax.ShapeDtypeStruct((1, slab, half), jnp.bfloat16),
        in_specs=[VMEM, ARRIVED],
        out_specs=HBM,
        scratch_shapes=[
            pltpu.VMEM((slab, half), jnp.bfloat16),
            pltpu.VMEM((slab, half), jnp.bfloat16),
            pltpu.SemaphoreType.DMA((STEPS,)),
            pltpu.SemaphoreType.DMA((STEPS,)),
        ],
        cost_estimate=cost(ADDCOST),
        compiler_params=params(),
        name="add",
    )(keep, arrived)
    return (weight_out, gboth + there)


def solution(mesh):
    return jax.shard_map(
        local,
        mesh=mesh,
        in_specs=(
            P("pipe", None, GROUP, None),
            P("pipe", None, GROUP, None),
            P("pipe", GROUP, None),
            P("pipe", "fsdp", None),
            P("pipe", "fsdp"),
        ),
        out_specs=(P("pipe", GROUP, None), P("pipe", "fsdp")),
        check_vma=False,
    )
```

```python
import functools

import jax
import jax.numpy as jnp
from jax import lax
from jax.experimental import pallas as pl
from jax.experimental.pallas import tpu as pltpu
from jax.sharding import PartitionSpec as P

GROUP = ("fsdp", "dp")
TILE = 256
BAND = 128
SPLIT = 80
STEPS = 4
EPS = 1e-05
ADDCOST = 1 << 20
VLIM = 20
HBM = pl.BlockSpec(memory_space=pltpu.HBM)
VMEM = pl.BlockSpec(memory_space=pltpu.VMEM)
SMEM = pl.BlockSpec(memory_space=pltpu.SMEM)
ARRIVED = pl.BlockSpec(memory_space=pl.ANY)


def params():
    return pltpu.CompilerParams(vmem_limit_bytes=VLIM << 20)


def cost(size=0):
    return pl.CostEstimate(flops=0, bytes_accessed=size, transcendentals=0)


def split_kernel(
    order_ref, upper_ref, acts_ref, cot_ref, first_ref, second_ref, acts_own, cot_own, acts_sem, cot_sem
):
    groups = first_ref.shape[0]
    _, batches, tokens, width = acts_ref.shape
    slab = width // groups
    half = cot_ref.shape[-1] // 2
    copies = [pltpu.make_async_copy(acts_ref.at[0, m], acts_own.at[m], acts_sem.at[m]) for m in range(batches)]
    load_cot = pltpu.make_async_copy(cot_ref.at[0], cot_own, cot_sem)
    for load in copies:
        load.start()
    load_cot.start()
    keep_at = pl.multiple_of(upper_ref[0] * half, 128)
    send_at = pl.multiple_of((1 - upper_ref[0]) * half, 128)
    for m in range(batches):
        copies[m].wait()
        rows = slice(m * tokens, (m + 1) * tokens)
        squares = jnp.zeros((tokens, 128), jnp.float32)
        for c in range(0, width, 128):
            floats = acts_own[m, :, c : c + 128].astype(jnp.float32)
            squares += floats * floats
        rstd = lax.rsqrt(jnp.sum(squares, axis=-1, keepdims=True) / width + EPS)
        if m == 0:
            load_cot.wait()
        slot = jnp.int32(0)
        for j in range(1, batches):
            slot = jnp.where(order_ref[0, 0, j] == m, jnp.int32(j), slot)
        send = (cot_own[slot, :, pl.ds(send_at, half)].astype(jnp.float32) * rstd).astype(jnp.bfloat16)
        keep = (cot_own[slot, :, pl.ds(keep_at, half)].astype(jnp.float32) * rstd).astype(jnp.bfloat16)
        for q in range(groups):
            second_ref[q, rows, :] = keep
            first_ref[q, rows, :half] = send
            first_ref[q, rows, half:] = acts_own[m, :, q * slab : (q + 1) * slab]


def split(acts, cotangent, order, upper, groups):
    _, batches, tokens, width = acts.shape
    keys = cotangent.shape[-1]
    half = keys // 2
    sizes = (half + width // groups, half)
    acts, cotangent, order = (pltpu.with_memory_space_constraint(x, pltpu.HBM) for x in (acts, cotangent, order))
    return pl.pallas_call(
        split_kernel,
        out_shape=tuple(jax.ShapeDtypeStruct((groups, batches * tokens, n), jnp.bfloat16) for n in sizes),
        in_specs=[SMEM, SMEM, HBM, HBM],
        out_specs=(VMEM, VMEM),
        scratch_shapes=[
            pltpu.VMEM((batches, tokens, width), jnp.bfloat16),
            pltpu.VMEM((batches, tokens, keys), jnp.bfloat16),
            pltpu.SemaphoreType.DMA((batches,)),
            pltpu.SemaphoreType.DMA,
        ],
        cost_estimate=cost(5 << 20),
        compiler_params=pltpu.CompilerParams(vmem_limit_bytes=SPLIT << 18),
        name="split",
    )(order, upper, acts, cotangent)


def half_product(block_ref, grads, at, half):
    return lax.dot_general(
        block_ref[:, half + at : half + at + TILE], grads, (((0,), (0,)), ((), ())), preferred_element_type=jnp.float32
    )


def gain_terms(total, weight):
    terms = total * weight.astype(jnp.float32)
    folded = terms[:, :128]
    for c in range(128, terms.shape[1], 128):
        folded += terms[:, c : c + 128]
    return jnp.sum(folded.T, axis=0, keepdims=True)


def fetch_weight(weight_ref, own_ref, sem, first, column):
    rows, half = own_ref.shape
    copy = pltpu.make_async_copy(weight_ref.at[0, pl.ds(first, rows), pl.ds(column, half)], own_ref, sem)
    copy.start()
    return copy


def scaled_kernel(replica_ref, grads_ref, block_ref, gain_ref, out_ref):
    rows, half = out_ref.shape
    first = pl.multiple_of(replica_ref[0] * rows, rows)
    grads = grads_ref[:, :half]
    for at in range(0, rows, TILE):
        gain = gain_ref[:, pl.ds(pl.multiple_of(first + at, 128), TILE)].reshape(TILE, 1)
        out_ref[at : at + TILE, :] = (half_product(block_ref, grads, at, half) * gain).astype(out_ref.dtype)


def send_kernel(replica_ref, block_ref, gain_ref, out_ref, own_ref, sem):
    rows, half = out_ref.shape
    first = pl.multiple_of(replica_ref[0] * rows, rows)
    grads = block_ref[:, :half]
    stores = []
    for at in range(0, rows, BAND):
        band = pl.ds(at, BAND)
        gain = gain_ref[:, pl.ds(pl.multiple_of(first + at, 128), BAND)].reshape(BAND, 1)
        total = lax.dot_general(
            block_ref[:, half + at : half + at + BAND], grads, (((0,), (0,)), ((), ())), preferred_element_type=jnp.float32
        )
        own_ref[band, :] = (total * gain).astype(out_ref.dtype)
        stores.append(pltpu.make_async_copy(own_ref.at[band], out_ref.at[band], sem.at[at // BAND]))
        stores[-1].start()
    for store in stores:
        store.wait()


def gain_kernel(keeping, upper_ref, replica_ref, grads_ref, block_ref, weight_ref, *refs):
    before, (gterm_ref, own_ref, total_ref, sem) = refs[:keeping], refs[keeping:]
    rows, half = own_ref.shape
    first = pl.multiple_of(replica_ref[0] * rows, rows)
    side = upper_ref[0] if keeping else 1 - upper_ref[0]
    fetch = fetch_weight(weight_ref, own_ref, sem, first, pl.multiple_of(side * half, half))
    if keeping:
        gterm_ref[...] = jnp.zeros_like(gterm_ref)
    grads = grads_ref[:, :half]
    for at in range(0, rows, TILE):
        total_ref[at : at + TILE, :] = half_product(block_ref, grads, at, half)
    fetch.wait()
    for at in range(0, rows, TILE):
        gterm = gain_terms(total_ref[at : at + TILE, :], own_ref[at : at + TILE, :])
        if keeping:
            where = pl.ds(pl.multiple_of(first + at, 128), TILE)
            gterm_ref[:, where] = gterm + before[0][:, at : at + TILE]
        else:
            gterm_ref[:, at : at + TILE] = gterm


def add_kernel(keep_ref, arrived_ref, out_ref, arrived_own, out_own, load_sem, store_sem):
    rows = keep_ref.shape[0] // STEPS
    bands = [pl.ds(n * rows, rows) for n in range(STEPS)]
    loads = [
        pltpu.make_async_copy(arrived_ref.at[band], arrived_own.at[band], load_sem.at[n]) for n, band in enumerate(bands)
    ]
    stores = [
        pltpu.make_async_copy(out_own.at[band], out_ref.at[0, band], store_sem.at[n]) for n, band in enumerate(bands)
    ]
    for load in loads:
        load.start()
    for band, load, store in zip(bands, loads, stores):
        load.wait()
        out_own[band, :] = (keep_ref[band, :] + arrived_own[band, :].astype(jnp.float32)).astype(jnp.bfloat16)
        store.start()
    for store in stores:
        store.wait()


def local(acts, cotangent, order, key_weight, gain):
    groups = lax.axis_size(GROUP)
    slab = acts.shape[-1] // groups
    tokens = acts.shape[1] * acts.shape[2]
    half = cotangent.shape[-1] // 2
    ranks = lax.axis_size("pipe")
    middle = ranks // 2
    upper = (lax.axis_index("pipe") >= middle).astype(jnp.int32).reshape(1)
    replica = lax.axis_index("dp").reshape(1)
    across = [(i, (i + middle) % ranks) for i in range(ranks)]

    def exchange(block):
        return lax.all_to_all(block, GROUP, 0, 0, tiled=True).reshape(groups * tokens, -1)

    key_weight = pltpu.with_memory_space_constraint(key_weight, pltpu.HBM)
    first, second = split(acts, cotangent, order, upper, groups)
    block = exchange(first)
    second, block = lax.optimization_barrier((second, block))
    grads = exchange(second)
    scratch = [
        pltpu.VMEM((slab, half), jnp.bfloat16),
        pltpu.VMEM((slab, half), jnp.float32),
        pltpu.SemaphoreType.DMA,
    ]

    def scaled(grads, kind, name):
        return pl.pallas_call(
            scaled_kernel,
            out_shape=jax.ShapeDtypeStruct((slab, half), kind),
            in_specs=[SMEM, VMEM, VMEM, VMEM],
            out_specs=VMEM,
            cost_estimate=cost(),
            compiler_params=params(),
            name=name,
        )(replica, grads, block, gain)

    def gain_part(grads, *before):
        return pl.pallas_call(
            functools.partial(gain_kernel, len(before)),
            out_shape=jax.ShapeDtypeStruct(gain.shape if before else (1, slab), jnp.float32),
            in_specs=[SMEM, SMEM, VMEM, VMEM, HBM] + [VMEM] * len(before),
            out_specs=VMEM,
            scratch_shapes=scratch,
            cost_estimate=cost(),
            compiler_params=params(),
            name="gain",
        )(upper, replica, grads, block, key_weight, *before)

    send = pl.pallas_call(
        send_kernel,
        out_shape=jax.ShapeDtypeStruct((slab, half), jnp.bfloat16),
        in_specs=[SMEM, VMEM, VMEM],
        out_specs=HBM,
        scratch_shapes=[pltpu.VMEM((slab, half), jnp.bfloat16), pltpu.SemaphoreType.DMA((slab // BAND,))],
        cost_estimate=cost(),
        compiler_params=params(),
        name="send",
    )(replica, block, gain)
    arrived = lax.ppermute(send, "pipe", across)
    gown = gain_part(grads, gain_part(block))
    gboth = lax.psum(gown, "dp")
    there = lax.ppermute(gboth, "pipe", across)
    late_grads, _ = lax.optimization_barrier((grads, gboth))
    keep = scaled(late_grads, jnp.float32, "keep")
    weight_out = (keep + arrived.astype(jnp.float32)).astype(jnp.bfloat16)[None]
    return (weight_out, gboth + there)


def solution(mesh):
    return jax.shard_map(
        local,
        mesh=mesh,
        in_specs=(
            P("pipe", None, GROUP, None),
            P("pipe", None, GROUP, None),
            P("pipe", GROUP, None),
            P("pipe", "fsdp", None),
            P("pipe", "fsdp"),
        ),
        out_specs=(P("pipe", GROUP, None), P("pipe", "fsdp")),
        check_vma=False,
    )
```

```python
import functools

import jax
import jax.numpy as jnp
from jax import lax
from jax.experimental import pallas as pl
from jax.experimental.pallas import tpu as pltpu
from jax.sharding import PartitionSpec as P

GROUP = ("fsdp", "dp")
TILE = 256
BAND = 128
SPLIT = 80
STEPS = 4
EPS = 1e-05
ADDCOST = 1 << 20
VLIM = 20
HBM = pl.BlockSpec(memory_space=pltpu.HBM)
VMEM = pl.BlockSpec(memory_space=pltpu.VMEM)
SMEM = pl.BlockSpec(memory_space=pltpu.SMEM)
ARRIVED = pl.BlockSpec(memory_space=pl.ANY)


def params():
    return pltpu.CompilerParams(vmem_limit_bytes=VLIM << 20)


def cost(size=0):
    return pl.CostEstimate(flops=0, bytes_accessed=size, transcendentals=0)


def split_kernel(
    order_ref, upper_ref, acts_ref, cot_ref, first_ref, second_ref, acts_own, cot_own, acts_sem, cot_sem
):
    groups = first_ref.shape[0]
    _, batches, tokens, width = acts_ref.shape
    slab = width // groups
    half = cot_ref.shape[-1] // 2
    copies = [pltpu.make_async_copy(acts_ref.at[0, m], acts_own.at[m], acts_sem.at[m]) for m in range(batches)]
    load_cot = pltpu.make_async_copy(cot_ref.at[0], cot_own, cot_sem)
    for load in copies:
        load.start()
    load_cot.start()
    keep_at = pl.multiple_of(upper_ref[0] * half, 128)
    send_at = pl.multiple_of((1 - upper_ref[0]) * half, 128)
    for m in range(batches):
        copies[m].wait()
        rows = slice(m * tokens, (m + 1) * tokens)
        squares = jnp.zeros((tokens, 128), jnp.float32)
        for c in range(0, width, 128):
            floats = acts_own[m, :, c : c + 128].astype(jnp.float32)
            squares += floats * floats
        rstd = lax.rsqrt(jnp.sum(squares, axis=-1, keepdims=True) / width + EPS)
        if m == 0:
            load_cot.wait()
        slot = jnp.int32(0)
        for j in range(1, batches):
            slot = jnp.where(order_ref[0, 0, j] == m, jnp.int32(j), slot)
        send = (cot_own[slot, :, pl.ds(send_at, half)].astype(jnp.float32) * rstd).astype(jnp.bfloat16)
        keep = (cot_own[slot, :, pl.ds(keep_at, half)].astype(jnp.float32) * rstd).astype(jnp.bfloat16)
        for q in range(groups):
            second_ref[q, rows, :] = keep
            first_ref[q, rows, :half] = send
            first_ref[q, rows, half:] = acts_own[m, :, q * slab : (q + 1) * slab]


def split(acts, cotangent, order, upper, groups):
    _, batches, tokens, width = acts.shape
    keys = cotangent.shape[-1]
    half = keys // 2
    sizes = (half + width // groups, half)
    acts, cotangent, order = (pltpu.with_memory_space_constraint(x, pltpu.HBM) for x in (acts, cotangent, order))
    return pl.pallas_call(
        split_kernel,
        out_shape=tuple(jax.ShapeDtypeStruct((groups, batches * tokens, n), jnp.bfloat16) for n in sizes),
        in_specs=[SMEM, SMEM, HBM, HBM],
        out_specs=(VMEM, VMEM),
        scratch_shapes=[
            pltpu.VMEM((batches, tokens, width), jnp.bfloat16),
            pltpu.VMEM((batches, tokens, keys), jnp.bfloat16),
            pltpu.SemaphoreType.DMA((batches,)),
            pltpu.SemaphoreType.DMA,
        ],
        cost_estimate=cost(5 << 20),
        compiler_params=pltpu.CompilerParams(vmem_limit_bytes=SPLIT << 18),
        name="split",
    )(order, upper, acts, cotangent)


def half_product(block_ref, grads, at, half):
    return lax.dot_general(
        block_ref[:, half + at : half + at + TILE], grads, (((0,), (0,)), ((), ())), preferred_element_type=jnp.float32
    )


def gain_terms(total, weight):
    terms = total * weight.astype(jnp.float32)
    folded = terms[:, :128]
    for c in range(128, terms.shape[1], 128):
        folded += terms[:, c : c + 128]
    return jnp.sum(folded.T, axis=0, keepdims=True)


def fetch_weight(weight_ref, own_ref, sem, first, column):
    rows, half = own_ref.shape
    copy = pltpu.make_async_copy(weight_ref.at[0, pl.ds(first, rows), pl.ds(column, half)], own_ref, sem)
    copy.start()
    return copy


def scaled_kernel(replica_ref, grads_ref, block_ref, gain_ref, out_ref):
    rows, half = out_ref.shape
    first = pl.multiple_of(replica_ref[0] * rows, rows)
    grads = grads_ref[:, :half]
    for at in range(0, rows, TILE):
        gain = gain_ref[:, pl.ds(pl.multiple_of(first + at, 128), TILE)].reshape(TILE, 1)
        out_ref[at : at + TILE, :] = (half_product(block_ref, grads, at, half) * gain).astype(out_ref.dtype)


def send_kernel(replica_ref, block_ref, gain_ref, out_ref, own_ref, sem):
    rows, half = out_ref.shape
    first = pl.multiple_of(replica_ref[0] * rows, rows)
    grads = block_ref[:, :half]
    stores = []
    for at in range(0, rows, BAND):
        band = pl.ds(at, BAND)
        gain = gain_ref[:, pl.ds(pl.multiple_of(first + at, 128), BAND)].reshape(BAND, 1)
        total = lax.dot_general(
            block_ref[:, half + at : half + at + BAND], grads, (((0,), (0,)), ((), ())), preferred_element_type=jnp.float32
        )
        own_ref[band, :] = (total * gain).astype(out_ref.dtype)
        stores.append(pltpu.make_async_copy(own_ref.at[band], out_ref.at[band], sem.at[at // BAND]))
        stores[-1].start()
    for store in stores:
        store.wait()


def gain_kernel(keeping, upper_ref, replica_ref, grads_ref, block_ref, weight_ref, *refs):
    before, (gterm_ref, own_ref, total_ref, sem) = refs[:keeping], refs[keeping:]
    rows, half = own_ref.shape
    first = pl.multiple_of(replica_ref[0] * rows, rows)
    side = upper_ref[0] if keeping else 1 - upper_ref[0]
    fetch = fetch_weight(weight_ref, own_ref, sem, first, pl.multiple_of(side * half, half))
    if keeping:
        gterm_ref[...] = jnp.zeros_like(gterm_ref)
    grads = grads_ref[:, :half]
    for at in range(0, rows, TILE):
        total_ref[at : at + TILE, :] = half_product(block_ref, grads, at, half)
    fetch.wait()
    for at in range(0, rows, TILE):
        gterm = gain_terms(total_ref[at : at + TILE, :], own_ref[at : at + TILE, :])
        if keeping:
            where = pl.ds(pl.multiple_of(first + at, 128), TILE)
            gterm_ref[:, where] = gterm + before[0][:, at : at + TILE]
        else:
            gterm_ref[:, at : at + TILE] = gterm


def add_kernel(keep_ref, arrived_ref, out_ref, arrived_own, out_own, load_sem, store_sem):
    rows = keep_ref.shape[0] // STEPS
    bands = [pl.ds(n * rows, rows) for n in range(STEPS)]
    loads = [
        pltpu.make_async_copy(arrived_ref.at[band], arrived_own.at[band], load_sem.at[n]) for n, band in enumerate(bands)
    ]
    stores = [
        pltpu.make_async_copy(out_own.at[band], out_ref.at[0, band], store_sem.at[n]) for n, band in enumerate(bands)
    ]
    for load in loads:
        load.start()
    for band, load, store in zip(bands, loads, stores):
        load.wait()
        out_own[band, :] = (keep_ref[band, :] + arrived_own[band, :].astype(jnp.float32)).astype(jnp.bfloat16)
        store.start()
    for store in stores:
        store.wait()


def local(acts, cotangent, order, key_weight, gain):
    groups = lax.axis_size(GROUP)
    slab = acts.shape[-1] // groups
    tokens = acts.shape[1] * acts.shape[2]
    half = cotangent.shape[-1] // 2
    ranks = lax.axis_size("pipe")
    middle = ranks // 2
    upper = (lax.axis_index("pipe") >= middle).astype(jnp.int32).reshape(1)
    replica = lax.axis_index("dp").reshape(1)
    across = [(i, (i + middle) % ranks) for i in range(ranks)]

    def exchange(block):
        return lax.all_to_all(block, GROUP, 0, 0, tiled=True).reshape(groups * tokens, -1)

    key_weight = pltpu.with_memory_space_constraint(key_weight, pltpu.HBM)
    first, second = split(acts, cotangent, order, upper, groups)
    block = exchange(first)
    second, block = lax.optimization_barrier((second, block))
    grads = exchange(second)
    scratch = [
        pltpu.VMEM((slab, half), jnp.bfloat16),
        pltpu.VMEM((slab, half), jnp.float32),
        pltpu.SemaphoreType.DMA,
    ]

    def scaled(grads, kind, name):
        return pl.pallas_call(
            scaled_kernel,
            out_shape=jax.ShapeDtypeStruct((slab, half), kind),
            in_specs=[SMEM, VMEM, VMEM, VMEM],
            out_specs=VMEM,
            cost_estimate=cost(),
            compiler_params=params(),
            name=name,
        )(replica, grads, block, gain)

    def gain_part(grads, *before):
        return pl.pallas_call(
            functools.partial(gain_kernel, len(before)),
            out_shape=jax.ShapeDtypeStruct(gain.shape if before else (1, slab), jnp.float32),
            in_specs=[SMEM, SMEM, VMEM, VMEM, HBM] + [VMEM] * len(before),
            out_specs=VMEM,
            scratch_shapes=scratch,
            cost_estimate=cost(),
            compiler_params=params(),
            name="gain",
        )(upper, replica, grads, block, key_weight, *before)

    send = pl.pallas_call(
        send_kernel,
        out_shape=jax.ShapeDtypeStruct((slab, half), jnp.bfloat16),
        in_specs=[SMEM, VMEM, VMEM],
        out_specs=HBM,
        scratch_shapes=[pltpu.VMEM((slab, half), jnp.bfloat16), pltpu.SemaphoreType.DMA((slab // BAND,))],
        cost_estimate=cost(),
        compiler_params=params(),
        name="send",
    )(replica, block, gain)
    arrived = lax.ppermute(send, "pipe", across)
    gown = gain_part(grads, gain_part(block))
    gboth = gown + lax.ppermute(gown, "dp", [(0, 1), (1, 0)])
    late_grads, _ = lax.optimization_barrier((grads, gown))
    keep = scaled(late_grads, jnp.float32, "keep")
    gboth, keep = lax.optimization_barrier((gboth, keep))
    there = lax.ppermute(gboth, "pipe", across)
    weight_out = (keep + arrived.astype(jnp.float32)).astype(jnp.bfloat16)[None]
    return (weight_out, gboth + there)


def solution(mesh):
    return jax.shard_map(
        local,
        mesh=mesh,
        in_specs=(
            P("pipe", None, GROUP, None),
            P("pipe", None, GROUP, None),
            P("pipe", GROUP, None),
            P("pipe", "fsdp", None),
            P("pipe", "fsdp"),
        ),
        out_specs=(P("pipe", GROUP, None), P("pipe", "fsdp")),
        check_vma=False,
    )
```
